32 devices in a mesh: site: 8 (over z, x), real: 4 (over y, core).
Axes of the slice: x: 2, y: 2, z: 4, core: 2. Of those that a mesh axis runs over, the one named last changes fastest.
Arguments:
- epsilon: bfloat16 [8192, 2048], P('site', 'real'), may hold values from -6 to 6
- factor: bfloat16 [2, 72, 512, 512], P(None, 'site'), may hold values from -0.09375 to 0.09375
- block_rows: int32 [2, 72], P(None, 'site'), may hold values from 0 to 15, as said below
- median_log: float32 [8192], P('site'), may hold values from -2.5 to -0.5
- spread_log: float32 [8192], P('site'), may hold values from 0.4 to 0.8
- critical_yield: float32 [8192], P('site'), may hold values from 0.03 to 0.3
Outputs:
- residual_field: bfloat16 [8192, 2048], P('site', 'real')
- mean_damage: float32 [8192], P('site')
The draws below stay inside these ranges and needn't reach their ends.
Inputs may be any that keep to these rules, and one draw needn't show every extreme that they name: block_rows[p, b] = (c + o) mod 16, with c = 2 * (b // 9) + p the block's column tile and o in 0 to 11; the offsets o of one block column are distinct, and the first block of each column has o = 0.
All inputs are finite; a program needn't handle non-finite values.
Results may differ from the reference program's by a relative error of at most 0.001.
Values sent between devices are 32-bit elements; how exact they have to be, the bound alone decides.
A program may use at most 256 MiB of HBM per device.

```python
import math
import jax
import jax.numpy as jnp
from jax import lax

TILE = 512
PANELS = 2
BLOCKS = 9
BAND = 12
TILES = 16
NBLK = 72
SITES = 8192
REALS = 2048


def draw_block_rows(key, part):
    columns = TILES // PANELS
    scores = jax.random.randint(key, (PANELS, columns, BAND - 1), 0, 1 << 20) * BAND
    scores = scores + jnp.arange(BAND - 1, dtype=jnp.int32)
    chosen = jnp.argsort(scores, axis=-1)[:, :, :BLOCKS - 1].astype(jnp.int32) + 1
    offsets = jnp.concatenate([jnp.zeros((PANELS, columns, 1), jnp.int32), chosen], axis=-1)
    column_tile = PANELS * jnp.arange(columns, dtype=jnp.int32)[None, :, None] + jnp.arange(PANELS, dtype=jnp.int32)[:, None, None]
    result = (column_tile + offsets) % TILES
    return result.reshape(PANELS, columns * BLOCKS).astype(jnp.int32)


def levels(rng, shape, pieces, least, high):
    level = 1.0
    for position, blocks in pieces:
        steps = jax.random.uniform(jax.random.fold_in(jax.random.fold_in(rng, 6), position), (blocks,), jnp.float32, least / len(pieces), high / len(pieces))
        level = level * jnp.repeat(jnp.exp(steps), shape[position] // blocks).reshape((-1,) + (1,) * (len(shape) - 1 - position))
    return level


def centred(own_key, extent, spread, most, cuts=(), kind=jnp.bfloat16):
    gain = levels(own_key, extent, cuts, -0.22, 0.18) if cuts else 1.0
    drawn = jax.random.normal(own_key, extent, jnp.float32) * spread * gain
    return jnp.minimum(jnp.maximum(drawn, -most), most).astype(kind)


def setup_inputs(seed: int = 0) -> dict:
    streams_of = jax.random.split(jax.random.key(seed), 7)
    return {
        "epsilon": centred(streams_of[0], (SITES, REALS), 1.0, 6.0, ((0, 8), (1, 4))),
        "factor": centred(streams_of[1], (PANELS, NBLK, TILE, TILE), (TILE * BLOCKS) ** -0.5, 0.09375, ((1, 8),)),
        "block_rows": draw_block_rows(jax.random.fold_in(streams_of[6], 71), 0),
        "median_log": jnp.clip(-2.5 + 2.0 * jax.random.uniform(streams_of[3], (SITES,), jnp.float32) ** levels(streams_of[3], (SITES,), ((0, 8),), -0.2, 0.2), -2.5, -0.5),
        "spread_log": jnp.clip(0.4 + 0.4 * jax.random.uniform(streams_of[4], (SITES,), jnp.float32) ** levels(streams_of[4], (SITES,), ((0, 8),), -0.2, 0.2), 0.4, 0.8),
        "critical_yield": jnp.clip(jnp.exp(math.log(0.3) - 2.3025852 * jax.random.uniform(streams_of[5], (SITES,), jnp.float32) ** levels(streams_of[5], (SITES,), ((0, 8),), -0.2, 0.2)), 0.03, 0.3),
    }


coeff_disp = 10.0 ** 0.215
power_margin = 2.341
power_ratio = 1.438


def reference(epsilon, factor, block_rows, median_log, spread_log, critical_yield):
    tiles = SITES // TILE
    draws = epsilon.reshape(tiles, TILE, REALS)
    field = jnp.zeros((tiles, TILE, REALS), jnp.float32)
    for panel in range(PANELS):
        def add_block(carry, item):
            block, target, number = item
            column = (PANELS * (number // BLOCKS) + panel).astype(jnp.int32)
            source = lax.dynamic_index_in_dim(draws, column, 0, keepdims=False)
            product = jnp.dot(block, source, preferred_element_type=jnp.float32)
            return carry.at[target].add(product), None
        numbers = jnp.arange(NBLK, dtype=jnp.int32)
        field, unused = lax.scan(add_block, field, (factor[panel], block_rows[panel], numbers))
    residual_field = field.astype(jnp.bfloat16).reshape(SITES, REALS)
    log_peak = median_log[:, None] + spread_log[:, None] * residual_field.astype(jnp.float32)
    log_ratio = jnp.log(critical_yield)[:, None] - log_peak
    ratio = jnp.exp(log_ratio)
    margin = jnp.maximum(1.0 - ratio, 0.0)
    displacement = coeff_disp * jnp.power(margin, power_margin) * jnp.exp(-power_ratio * log_ratio)
    mean_damage = jnp.sum(jnp.log1p(displacement), axis=1) / REALS
    return residual_field, mean_damage
```

```python
import functools
import jax
import jax.numpy as jnp
from jax import lax
from jax.experimental import pallas as pl
from jax.experimental.pallas import tpu as pltpu
from jax.sharding import PartitionSpec as P

BAND = 12
PAIR = 2
ROWS = 128
AHEAD = 24
LAG = 1
MESH = pl.DeviceIdType.MESH

coeff_disp = 10.0**0.215
power_margin = 2.341
power_ratio = 1.438


def passed_along(value, axis, steps):
    count = lax.axis_size(axis)
    pairs = [(source, (source + steps) % count) for source in range(count)]
    return lax.ppermute(value, axis, pairs)


def shards(epsilon, factor, block_rows, median_log, spread_log, critical_yield):
    panels = factor.shape[0]
    per_column = factor.shape[1]
    tile_size = factor.shape[-1]
    own_reals = epsilon.shape[1]
    reach = BAND // 2
    own_index = lax.axis_index("site")
    total_tiles = panels * lax.axis_size("site")
    draws = epsilon.reshape(panels, tile_size, own_reals)

    def pending(panel):
        flat = factor[panel].reshape(per_column * tile_size, tile_size)
        products = jnp.dot(flat, draws[panel], preferred_element_type=jnp.float32)
        products = products.reshape(per_column, tile_size, own_reals)
        relative = (block_rows[panel] - own_index * panels) % total_tiles
        slots = jnp.zeros(((reach + 1) * panels, tile_size, own_reals), jnp.float32)
        sums = slots.at[relative].set(products, unique_indices=True)
        return sums.reshape(reach + 1, panels, tile_size, own_reals)

    combined = pending(0)
    panel = 1
    combined = combined + pending(panel)
    arrived = combined[0]
    for offset in range(1, reach + 1):
        arrived = arrived + passed_along(combined[offset], "site", offset)
    residual_field = arrived.astype(jnp.bfloat16).reshape(panels * tile_size, own_reals)
    log_peak = median_log[:, None] + spread_log[:, None] * residual_field.astype(jnp.float32)
    log_ratio = jnp.log(critical_yield)[:, None] - log_peak
    ratio = jnp.exp(log_ratio)
    margin = jnp.maximum(1.0 - ratio, 0.0)
    displacement = coeff_disp * jnp.power(margin, power_margin) * jnp.exp(-power_ratio * log_ratio)
    local_total = jnp.sum(jnp.log1p(displacement), axis=1)
    total = lax.psum(local_total, "real")
    mean_damage = total / (own_reals * lax.axis_size("real"))
    return (residual_field, mean_damage)


def field_kernel(
    depth, own_reals, table, eps_in, factor_in, median, spread, critical, field_out, mean_out,
    eps, factor, x_out, x_in, z_out, z_in, totals,
    load_sem, x_send, x_recv, z_send, z_recv, t_send, t_recv,
):
    panels, per_column, tile = factor.shape[0], factor.shape[1], factor.shape[2]
    chunks = panels * tile // ROWS
    per_tile = tile // ROWS
    stages = depth - 1
    steps = stages * chunks
    reals = lax.axis_size("real")
    site = lax.axis_index("site")
    me = lax.axis_index("real")
    z, x = site // PAIR, site % PAIR

    loads = [pltpu.make_async_copy(eps_in, eps, load_sem.at[0])]
    for panel in range(panels):
        loads.append(pltpu.make_async_copy(factor_in.at[panel], factor.at[panel], load_sem.at[1 + panel]))
    for load in loads:
        load.start()

    barrier = pltpu.get_barrier_semaphore()
    pl.semaphore_signal(barrier, inc=1, device_id={"site": site + 1 - 2 * x}, device_id_type=MESH)
    for shift in range(1, reals):
        pl.semaphore_signal(barrier, inc=1, device_id={"real": (me + shift) % reals}, device_id_type=MESH)

    @pl.when(z > 0)
    def _():
        pl.semaphore_signal(barrier, inc=1, device_id={"site": site - PAIR}, device_id_type=MESH)

    @pl.when(z < depth - 1)
    def _():
        pl.semaphore_signal(barrier, inc=1, device_id={"site": site + PAIR}, device_id_type=MESH)

    pl.semaphore_wait(barrier, reals + jnp.where(z > 0, 1, 0) + jnp.where(z < depth - 1, 1, 0))

    for load in loads:
        load.wait()

    def partial(offset, chunk):
        relative = panels * offset + chunk // per_tile
        row = pl.multiple_of((chunk % per_tile) * ROWS, ROWS)
        result = None
        for panel in range(panels):
            block = factor[panel, table[panel, relative], pl.ds(row, ROWS), :]
            product = jnp.dot(
                block, eps[panel * tile:(panel + 1) * tile, :], preferred_element_type=jnp.float32
            ) * table[panels + panel, relative].astype(jnp.float32)
            result = product if result is None else result + product
        return result

    low = 2 * z < depth

    def target(stage):
        falling = depth - 1 - stage
        of_low = jnp.where(falling > z, falling, stage - (depth - 1 - z))
        of_high = jnp.where(stage < z, stage, depth - 1 - (stage - z))
        of_stage = jnp.where(low, of_low, of_high)
        return jnp.where(stage == stages, z, of_stage)

    skipped = jnp.where(z == 0, 0, jnp.where(low, stages - 1, z - 1))

    def x_copy(group, chunk):
        return pltpu.make_async_remote_copy(
            src_ref=x_out.at[group, chunk],
            dst_ref=x_in.at[group, chunk],
            send_sem=x_send.at[group, chunk],
            recv_sem=x_recv.at[group, chunk],
            device_id={"site": site + 1 - 2 * x},
            device_id_type=MESH,
        )

    def group_of(turn):
        return jnp.where(x == 0, jnp.where(turn >= skipped, turn + 1, turn), turn)

    def x_step(step):
        group, chunk = group_of(step // chunks), step % chunks
        offset = (PAIR * (target(group) - z + depth) + 1 - 2 * x) % (PAIR * depth)
        x_out[group, chunk] = partial(offset, chunk)
        x_copy(group, chunk).start()

    def z_copy(side, dest, chunk, stage, there):
        return pltpu.make_async_remote_copy(
            src_ref=z_out.at[stage, chunk],
            dst_ref=z_in.at[side, dest, chunk],
            send_sem=z_send.at[stage, chunk],
            recv_sem=z_recv.at[side, dest, chunk],
            device_id={"site": there},
            device_id_type=MESH,
        )

    def arrived(side, dest, chunk):
        z_copy(side, dest, chunk, 0, (site + PAIR) % (PAIR * depth)).wait_recv()
        return z_in[side, dest, chunk]

    def z_step(step):
        stage, chunk = step // chunks, step % chunks
        dest = target(stage)
        up = dest > z
        side = jnp.where(up, 0, 1)
        offset = PAIR * ((dest - z + depth) % depth)
        z_out[stage, chunk] = partial(offset, chunk)

        @pl.when(jnp.logical_or(x == 0, stage != skipped))
        def _():
            x_copy(stage, chunk).wait_recv()
            z_out[stage, chunk] = z_out[stage, chunk] + x_in[stage, chunk]

        @pl.when(jnp.where(up, z, depth - 1 - z) > 0)
        def _():
            z_out[stage, chunk] = z_out[stage, chunk] + arrived(side, dest, chunk)

        z_copy(side, dest, chunk, stage, jnp.where(up, site + PAIR, site - PAIR)).start()

    def last_step(chunk):
        spare = z_out.at[stages, 0]
        spare[...] = partial(0, chunk)

        @pl.when(x == 1)
        def _():
            x_copy(stages, chunk).wait_recv()
            spare[...] = spare[...] + x_in[stages, chunk]

        @pl.when(z > 0)
        def _():
            spare[...] = spare[...] + arrived(0, z, chunk)

        @pl.when(z < depth - 1)
        def _():
            spare[...] = spare[...] + arrived(1, z, chunk)

        rounded = spare[...].astype(jnp.bfloat16)
        field_out[pl.ds(pl.multiple_of(chunk * ROWS, ROWS), ROWS), :] = rounded

        def column(ref):
            line = ref[pl.ds(chunk, 1), :]
            return jnp.broadcast_to(line, (ROWS, ROWS)).T[:, :1]

        log_yield = jnp.log(column(critical))
        log_peak = column(median) + column(spread) * rounded.astype(jnp.float32)
        log_ratio = log_yield - log_peak
        margin = jnp.maximum(1.0 - jnp.exp(log_ratio), 0.0)
        displacement = coeff_disp * jnp.exp(power_margin * jnp.log(margin) - power_ratio * log_ratio)
        damage = jnp.log1p(displacement)
        folded = damage[:, :ROWS]
        for piece in range(1, own_reals // ROWS):
            folded = folded + damage[:, piece * ROWS:(piece + 1) * ROWS]
        totals[me, pl.ds(chunk, 1), :] = jnp.sum(folded.T, axis=0, keepdims=True)

    @pl.loop(0, min(AHEAD, steps))
    def _(step):
        x_step(step)

    @pl.loop(0, steps)
    def _(step):
        if AHEAD < steps:
            @pl.when(step + AHEAD < steps)
            def _():
                x_step(step + AHEAD)

        z_step(step)

        @pl.when(step >= steps - chunks + LAG)
        def _():
            last_step(step - (steps - chunks + LAG))

    @pl.loop(chunks - LAG, chunks)
    def _(chunk):
        last_step(chunk)

    def t_copy(shift):
        return pltpu.make_async_remote_copy(
            src_ref=totals.at[me],
            dst_ref=totals.at[me],
            send_sem=t_send.at[shift],
            recv_sem=t_recv.at[shift],
            device_id={"real": (me + shift) % reals},
            device_id_type=MESH,
        )

    for shift in range(1, reals):
        t_copy(shift).start()

    @pl.loop(0, steps)
    def _(step):
        x_copy(group_of(step // chunks), step % chunks).wait_send()
        z_copy(0, 0, step % chunks, step // chunks, (site + PAIR) % (PAIR * depth)).wait_send()

    for shift in range(1, reals):
        t_copy(shift).wait()
    total = totals[0]
    for source in range(1, reals):
        total = total + totals[source]
    mean_out[...] = total / (own_reals * reals)


def line_shards(epsilon, factor, block_rows, median_log, spread_log, critical_yield):
    panels, per_column, tile = factor.shape[:3]
    sites, own_reals = epsilon.shape
    count, reals = lax.axis_size("site"), lax.axis_size("real")
    depth = count // PAIR
    chunks = sites // ROWS
    relative = (block_rows - lax.axis_index("site") * panels) % (panels * count)
    slots = jnp.arange((BAND // 2 + 1) * panels, dtype=jnp.int32)
    hits = (relative[:, :, None] == slots).astype(jnp.int32)
    numbers = jnp.arange(per_column, dtype=jnp.int32)[None, :, None]
    table = jnp.concatenate([jnp.sum(hits * numbers, axis=1), jnp.sum(hits, axis=1)], axis=0)
    piece = (ROWS, own_reals)
    vmem = pl.BlockSpec(memory_space=pltpu.VMEM)
    anywhere = pl.BlockSpec(memory_space=pl.ANY)
    field, mean = pl.pallas_call(
        functools.partial(field_kernel, depth, own_reals),
        out_shape=(
            jax.ShapeDtypeStruct((sites, own_reals), jnp.bfloat16),
            jax.ShapeDtypeStruct((chunks, ROWS), jnp.float32),
        ),
        in_specs=[pl.BlockSpec(memory_space=pltpu.SMEM), anywhere, anywhere, vmem, vmem, vmem],
        out_specs=(vmem, vmem),
        scratch_shapes=[
            pltpu.VMEM(epsilon.shape, epsilon.dtype),
            pltpu.VMEM(factor.shape, factor.dtype),
            pltpu.VMEM((depth, chunks) + piece, jnp.float32),
            pltpu.VMEM((depth, chunks) + piece, jnp.float32),
            pltpu.VMEM((depth, chunks) + piece, jnp.float32),
            pltpu.VMEM((2, depth, chunks) + piece, jnp.float32),
            pltpu.VMEM((reals, chunks, ROWS), jnp.float32),
            pltpu.SemaphoreType.DMA((1 + panels,)),
            pltpu.SemaphoreType.DMA((depth, chunks)),
            pltpu.SemaphoreType.DMA((depth, chunks)),
            pltpu.SemaphoreType.DMA((depth, chunks)),
            pltpu.SemaphoreType.DMA((2, depth, chunks)),
            pltpu.SemaphoreType.DMA((reals,)),
            pltpu.SemaphoreType.DMA((reals,)),
        ],
        compiler_params=pltpu.CompilerParams(
            collective_id=0, has_side_effects=True, vmem_limit_bytes=60 * 1024 * 1024
        ),
    )(
        table,
        epsilon,
        factor,
        median_log.reshape(chunks, ROWS),
        spread_log.reshape(chunks, ROWS),
        critical_yield.reshape(chunks, ROWS),
    )
    return field, mean.reshape(sites)


def solution(mesh):
    body = line_shards if mesh.shape["site"] == BAND // 2 + PAIR else shards
    return jax.shard_map(
        body,
        mesh=mesh,
        in_specs=(
            P("site", "real"),
            P(None, "site", None, None),
            P(None, "site"),
            P("site"),
            P("site"),
            P("site"),
        ),
        out_specs=(P("site", "real"), P("site")),
        check_vma=False,
    )
```

```python
import functools
import jax
import jax.numpy as jnp
from jax import lax
from jax.experimental import pallas as pl
from jax.experimental.pallas import tpu as pltpu
from jax.sharding import PartitionSpec as P

BAND = 12
PAIR = 2
ROWS = 128
AHEAD = 4
LAG = 1
MESH = pl.DeviceIdType.MESH

coeff_disp = 10.0**0.215
power_margin = 2.341
power_ratio = 1.438


def passed_along(value, axis, steps):
    count = lax.axis_size(axis)
    pairs = [(source, (source + steps) % count) for source in range(count)]
    return lax.ppermute(value, axis, pairs)


def shards(epsilon, factor, block_rows, median_log, spread_log, critical_yield):
    panels = factor.shape[0]
    per_column = factor.shape[1]
    tile_size = factor.shape[-1]
    own_reals = epsilon.shape[1]
    reach = BAND // 2
    own_index = lax.axis_index("site")
    total_tiles = panels * lax.axis_size("site")
    draws = epsilon.reshape(panels, tile_size, own_reals)

    def pending(panel):
        flat = factor[panel].reshape(per_column * tile_size, tile_size)
        products = jnp.dot(flat, draws[panel], preferred_element_type=jnp.float32)
        products = products.reshape(per_column, tile_size, own_reals)
        relative = (block_rows[panel] - own_index * panels) % total_tiles
        slots = jnp.zeros(((reach + 1) * panels, tile_size, own_reals), jnp.float32)
        sums = slots.at[relative].set(products, unique_indices=True)
        return sums.reshape(reach + 1, panels, tile_size, own_reals)

    combined = pending(0)
    panel = 1
    combined = combined + pending(panel)
    arrived = combined[0]
    for offset in range(1, reach + 1):
        arrived = arrived + passed_along(combined[offset], "site", offset)
    residual_field = arrived.astype(jnp.bfloat16).reshape(panels * tile_size, own_reals)
    log_peak = median_log[:, None] + spread_log[:, None] * residual_field.astype(jnp.float32)
    log_ratio = jnp.log(critical_yield)[:, None] - log_peak
    ratio = jnp.exp(log_ratio)
    margin = jnp.maximum(1.0 - ratio, 0.0)
    displacement = coeff_disp * jnp.power(margin, power_margin) * jnp.exp(-power_ratio * log_ratio)
    local_total = jnp.sum(jnp.log1p(displacement), axis=1)
    total = lax.psum(local_total, "real")
    mean_damage = total / (own_reals * lax.axis_size("real"))
    return (residual_field, mean_damage)


def field_kernel(
    depth, own_reals, table, eps_in, factor_in, median, spread, critical, field_out, mean_out,
    eps, factor, x_out, x_in, z_out, z_in, totals,
    load_sem, x_send, x_recv, z_send, z_recv, t_send, t_recv,
):
    panels, per_column, tile = factor.shape[0], factor.shape[1], factor.shape[2]
    chunks = panels * tile // ROWS
    per_tile = tile // ROWS
    stages = depth - 1
    steps = stages * chunks
    reals = lax.axis_size("real")
    site = lax.axis_index("site")
    me = lax.axis_index("real")
    z, x = site // PAIR, site % PAIR

    loads = [pltpu.make_async_copy(eps_in, eps, load_sem.at[0])]
    for panel in range(panels):
        loads.append(pltpu.make_async_copy(factor_in.at[panel], factor.at[panel], load_sem.at[1 + panel]))
    for load in loads:
        load.start()

    barrier = pltpu.get_barrier_semaphore()
    pl.semaphore_signal(barrier, inc=1, device_id={"site": site + 1 - 2 * x}, device_id_type=MESH)
    for shift in range(1, reals):
        pl.semaphore_signal(barrier, inc=1, device_id={"real": (me + shift) % reals}, device_id_type=MESH)

    @pl.when(z > 0)
    def _():
        pl.semaphore_signal(barrier, inc=1, device_id={"site": site - PAIR}, device_id_type=MESH)

    @pl.when(z < depth - 1)
    def _():
        pl.semaphore_signal(barrier, inc=1, device_id={"site": site + PAIR}, device_id_type=MESH)

    pl.semaphore_wait(barrier, reals + jnp.where(z > 0, 1, 0) + jnp.where(z < depth - 1, 1, 0))

    for load in loads:
        load.wait()

    def partial(offset, chunk):
        relative = panels * offset + chunk // per_tile
        row = pl.multiple_of((chunk % per_tile) * ROWS, ROWS)
        result = None
        for panel in range(panels):
            block = factor[panel, table[panel, relative], pl.ds(row, ROWS), :]
            product = jnp.dot(
                block, eps[panel * tile:(panel + 1) * tile, :], preferred_element_type=jnp.float32
            ) * table[panels + panel, relative].astype(jnp.float32)
            result = product if result is None else result + product
        return result

    low = 2 * z < depth

    def target(stage):
        falling = depth - 1 - stage
        of_low = jnp.where(falling > z, falling, stage - (depth - 1 - z))
        of_high = jnp.where(stage < z, stage, depth - 1 - (stage - z))
        of_stage = jnp.where(low, of_low, of_high)
        return jnp.where(stage == stages, z, of_stage)

    skipped = jnp.where(z == 0, 0, jnp.where(low, stages - 1, z - 1))

    def x_copy(group, chunk):
        return pltpu.make_async_remote_copy(
            src_ref=x_out.at[group, chunk],
            dst_ref=x_in.at[group, chunk],
            send_sem=x_send.at[group, chunk],
            recv_sem=x_recv.at[group, chunk],
            device_id={"site": site + 1 - 2 * x},
            device_id_type=MESH,
        )

    def group_of(turn):
        return jnp.where(x == 0, jnp.where(turn >= skipped, turn + 1, turn), turn)

    def x_step(step):
        group, chunk = group_of(step // chunks), step % chunks
        offset = (PAIR * (target(group) - z + depth) + 1 - 2 * x) % (PAIR * depth)
        x_out[group, chunk] = partial(offset, chunk)
        x_copy(group, chunk).start()

    def z_copy(side, dest, chunk, stage, there):
        return pltpu.make_async_remote_copy(
            src_ref=z_out.at[stage, chunk],
            dst_ref=z_in.at[side, dest, chunk],
            send_sem=z_send.at[stage, chunk],
            recv_sem=z_recv.at[side, dest, chunk],
            device_id={"site": there},
            device_id_type=MESH,
        )

    def arrived(side, dest, chunk):
        z_copy(side, dest, chunk, 0, (site + PAIR) % (PAIR * depth)).wait_recv()
        return z_in[side, dest, chunk]

    def z_step(step):
        stage, chunk = step // chunks, step % chunks
        dest = target(stage)
        up = dest > z
        side = jnp.where(up, 0, 1)
        offset = PAIR * ((dest - z + depth) % depth)
        z_out[stage, chunk] = partial(offset, chunk)

        @pl.when(jnp.logical_or(x == 0, stage != skipped))
        def _():
            x_copy(stage, chunk).wait_recv()
            z_out[stage, chunk] = z_out[stage, chunk] + x_in[stage, chunk]

        @pl.when(jnp.where(up, z, depth - 1 - z) > 0)
        def _():
            z_out[stage, chunk] = z_out[stage, chunk] + arrived(side, dest, chunk)

        z_copy(side, dest, chunk, stage, jnp.where(up, site + PAIR, site - PAIR)).start()

    def last_step(chunk):
        spare = z_out.at[stages, 0]
        spare[...] = partial(0, chunk)

        @pl.when(x == 1)
        def _():
            x_copy(stages, chunk).wait_recv()
            spare[...] = spare[...] + x_in[stages, chunk]

        @pl.when(z > 0)
        def _():
            spare[...] = spare[...] + arrived(0, z, chunk)

        @pl.when(z < depth - 1)
        def _():
            spare[...] = spare[...] + arrived(1, z, chunk)

        rounded = spare[...].astype(jnp.bfloat16)
        field_out[pl.ds(pl.multiple_of(chunk * ROWS, ROWS), ROWS), :] = rounded

        def column(ref):
            line = ref[pl.ds(chunk, 1), :]
            return jnp.broadcast_to(line, (ROWS, ROWS)).T[:, :1]

        log_yield = jnp.log(column(critical))
        log_peak = column(median) + column(spread) * rounded.astype(jnp.float32)
        log_ratio = log_yield - log_peak
        margin = jnp.maximum(1.0 - jnp.exp(log_ratio), 0.0)
        displacement = coeff_disp * jnp.exp(power_margin * jnp.log(margin) - power_ratio * log_ratio)
        damage = jnp.log1p(displacement)
        folded = damage[:, :ROWS]
        for piece in range(1, own_reals // ROWS):
            folded = folded + damage[:, piece * ROWS:(piece + 1) * ROWS]
        totals[me, pl.ds(chunk, 1), :] = jnp.sum(folded.T, axis=0, keepdims=True)

    @pl.loop(0, min(AHEAD, steps))
    def _(step):
        x_step(step)

    @pl.loop(0, steps)
    def _(step):
        if AHEAD < steps:
            @pl.when(step + AHEAD < steps)
            def _():
                x_step(step + AHEAD)

        z_step(step)

        @pl.when(step >= steps - chunks + LAG)
        def _():
            last_step(step - (steps - chunks + LAG))

    @pl.loop(chunks - LAG, chunks)
    def _(chunk):
        last_step(chunk)

    def t_copy(shift):
        return pltpu.make_async_remote_copy(
            src_ref=totals.at[me],
            dst_ref=totals.at[me],
            send_sem=t_send.at[shift],
            recv_sem=t_recv.at[shift],
            device_id={"real": (me + shift) % reals},
            device_id_type=MESH,
        )

    for shift in range(1, reals):
        t_copy(shift).start()

    @pl.loop(0, steps)
    def _(step):
        x_copy(group_of(step // chunks), step % chunks).wait_send()
        z_copy(0, 0, step % chunks, step // chunks, (site + PAIR) % (PAIR * depth)).wait_send()

    for shift in range(1, reals):
        t_copy(shift).wait()
    total = totals[0]
    for source in range(1, reals):
        total = total + totals[source]
    mean_out[...] = total / (own_reals * reals)


def line_shards(epsilon, factor, block_rows, median_log, spread_log, critical_yield):
    panels, per_column, tile = factor.shape[:3]
    sites, own_reals = epsilon.shape
    count, reals = lax.axis_size("site"), lax.axis_size("real")
    depth = count // PAIR
    chunks = sites // ROWS
    relative = (block_rows - lax.axis_index("site") * panels) % (panels * count)
    slots = jnp.arange((BAND // 2 + 1) * panels, dtype=jnp.int32)
    hits = (relative[:, :, None] == slots).astype(jnp.int32)
    numbers = jnp.arange(per_column, dtype=jnp.int32)[None, :, None]
    table = jnp.concatenate([jnp.sum(hits * numbers, axis=1), jnp.sum(hits, axis=1)], axis=0)
    piece = (ROWS, own_reals)
    vmem = pl.BlockSpec(memory_space=pltpu.VMEM)
    anywhere = pl.BlockSpec(memory_space=pl.ANY)
    field, mean = pl.pallas_call(
        functools.partial(field_kernel, depth, own_reals),
        out_shape=(
            jax.ShapeDtypeStruct((sites, own_reals), jnp.bfloat16),
            jax.ShapeDtypeStruct((chunks, ROWS), jnp.float32),
        ),
        in_specs=[pl.BlockSpec(memory_space=pltpu.SMEM), anywhere, anywhere, vmem, vmem, vmem],
        out_specs=(vmem, vmem),
        scratch_shapes=[
            pltpu.VMEM(epsilon.shape, epsilon.dtype),
            pltpu.VMEM(factor.shape, factor.dtype),
            pltpu.VMEM((depth, chunks) + piece, jnp.float32),
            pltpu.VMEM((depth, chunks) + piece, jnp.float32),
            pltpu.VMEM((depth, chunks) + piece, jnp.float32),
            pltpu.VMEM((2, depth, chunks) + piece, jnp.float32),
            pltpu.VMEM((reals, chunks, ROWS), jnp.float32),
            pltpu.SemaphoreType.DMA((1 + panels,)),
            pltpu.SemaphoreType.DMA((depth, chunks)),
            pltpu.SemaphoreType.DMA((depth, chunks)),
            pltpu.SemaphoreType.DMA((depth, chunks)),
            pltpu.SemaphoreType.DMA((2, depth, chunks)),
            pltpu.SemaphoreType.DMA((reals,)),
            pltpu.SemaphoreType.DMA((reals,)),
        ],
        compiler_params=pltpu.CompilerParams(
            collective_id=0, has_side_effects=True, vmem_limit_bytes=60 * 1024 * 1024
        ),
    )(
        table,
        epsilon,
        factor,
        median_log.reshape(chunks, ROWS),
        spread_log.reshape(chunks, ROWS),
        critical_yield.reshape(chunks, ROWS),
    )
    return field, mean.reshape(sites)


def solution(mesh):
    body = line_shards if mesh.shape["site"] == BAND // 2 + PAIR else shards
    return jax.shard_map(
        body,
        mesh=mesh,
        in_specs=(
            P("site", "real"),
            P(None, "site", None, None),
            P(None, "site"),
            P("site"),
            P("site"),
            P("site"),
        ),
        out_specs=(P("site", "real"), P("site")),
        check_vma=False,
    )
```

```python
import functools
import jax
import jax.numpy as jnp
from jax import lax
from jax.experimental import pallas as pl
from jax.experimental.pallas import tpu as pltpu
from jax.sharding import PartitionSpec as P

BAND = 12
PAIR = 2
LANES = 128
ROWS = 64
AHEAD = 6
PARTS = 4
HEAD = 2
LAG = 1
MESH = pl.DeviceIdType.MESH

coeff_disp = 10.0**0.215
power_margin = 2.341
power_ratio = 1.438


def passed_along(value, axis, steps):
    count = lax.axis_size(axis)
    pairs = [(source, (source + steps) % count) for source in range(count)]
    return lax.ppermute(value, axis, pairs)


def shards(epsilon, factor, block_rows, median_log, spread_log, critical_yield):
    panels = factor.shape[0]
    per_column = factor.shape[1]
    tile_size = factor.shape[-1]
    own_reals = epsilon.shape[1]
    reach = BAND // 2
    own_index = lax.axis_index("site")
    total_tiles = panels * lax.axis_size("site")
    draws = epsilon.reshape(panels, tile_size, own_reals)

    def pending(panel):
        flat = factor[panel].reshape(per_column * tile_size, tile_size)
        products = jnp.dot(flat, draws[panel], preferred_element_type=jnp.float32)
        products = products.reshape(per_column, tile_size, own_reals)
        relative = (block_rows[panel] - own_index * panels) % total_tiles
        slots = jnp.zeros(((reach + 1) * panels, tile_size, own_reals), jnp.float32)
        sums = slots.at[relative].set(products, unique_indices=True)
        return sums.reshape(reach + 1, panels, tile_size, own_reals)

    combined = pending(0)
    panel = 1
    combined = combined + pending(panel)
    arrived = combined[0]
    for offset in range(1, reach + 1):
        arrived = arrived + passed_along(combined[offset], "site", offset)
    residual_field = arrived.astype(jnp.bfloat16).reshape(panels * tile_size, own_reals)
    log_peak = median_log[:, None] + spread_log[:, None] * residual_field.astype(jnp.float32)
    log_ratio = jnp.log(critical_yield)[:, None] - log_peak
    ratio = jnp.exp(log_ratio)
    margin = jnp.maximum(1.0 - ratio, 0.0)
    displacement = coeff_disp * jnp.power(margin, power_margin) * jnp.exp(-power_ratio * log_ratio)
    local_total = jnp.sum(jnp.log1p(displacement), axis=1)
    total = lax.psum(local_total, "real")
    mean_damage = total / (own_reals * lax.axis_size("real"))
    return (residual_field, mean_damage)


def field_kernel(
    depth, own_reals, block_rows, eps_in, factor_in, median, spread, critical, field_out, mean_out,
    eps, factor, head, x_out, x_in, z_out, z_in, totals, columns, folds, table,
    load_sem, x_send, x_recv, z_send, z_recv, t_send, t_recv,
):
    panels, per_column, tile = factor.shape[0], factor.shape[1], factor.shape[2]
    chunks = panels * tile // ROWS
    per_tile = tile // ROWS
    stages = depth - 1
    steps = stages * chunks
    reals = lax.axis_size("real")
    site = lax.axis_index("site")
    me = lax.axis_index("real")
    z, x = site // PAIR, site % PAIR

    first = [pltpu.make_async_copy(eps_in, eps, load_sem.at[0])]
    rest = []
    for panel in range(panels):
        first.append(pltpu.make_async_copy(
            factor_in.at[panel, :, :head.shape[2], :], head.at[panel], load_sem.at[1 + panel]
        ))
        rest.append(pltpu.make_async_copy(
            factor_in.at[panel], factor.at[panel], load_sem.at[1 + panels + panel]
        ))
    for load in first + rest:
        load.start()

    barrier = pltpu.get_barrier_semaphore()
    pl.semaphore_signal(barrier, inc=1, device_id={"site": site + 1 - 2 * x}, device_id_type=MESH)
    for shift in range(1, reals):
        pl.semaphore_signal(barrier, inc=1, device_id={"real": (me + shift) % reals}, device_id_type=MESH)

    @pl.when(z > 0)
    def _():
        pl.semaphore_signal(barrier, inc=1, device_id={"site": site - PAIR}, device_id_type=MESH)

    @pl.when(z < depth - 1)
    def _():
        pl.semaphore_signal(barrier, inc=1, device_id={"site": site + PAIR}, device_id_type=MESH)

    for panel in range(panels):
        begins = [
            (block_rows[panel, block] - site * panels + panels * PAIR * depth) % (panels * PAIR * depth)
            for block in range(per_column)
        ]

        @pl.loop(0, table.shape[1])
        def _(slot):
            number, found = jnp.int32(0), jnp.int32(0)
            for block in range(per_column):
                hit = begins[block] == slot
                number = jnp.where(hit, block, number)
                found = jnp.where(hit, 1, found)
            table[panel, slot] = number
            table[panels + panel, slot] = found

    for index, ref in enumerate((median, spread, critical)):
        for line in range(panels * tile // LANES):
            spot = slice(line * LANES, (line + 1) * LANES)
            value = ref[line:line + 1, :]
            value = jnp.log(value) if index == 2 else value
            columns[index, spot, :] = jnp.broadcast_to(value, (LANES, LANES)).T

    pl.semaphore_wait(barrier, reals + jnp.where(z > 0, 1, 0) + jnp.where(z < depth - 1, 1, 0))

    for load in first:
        load.wait()

    def partial(offset, chunk, source=factor):
        relative = panels * offset + chunk // per_tile
        row = pl.multiple_of((chunk % per_tile) * ROWS, ROWS)
        result = None
        for panel in range(panels):
            block = source[panel, table[panel, relative], pl.ds(row, ROWS), :]
            product = jnp.dot(
                block, eps[panel * tile:(panel + 1) * tile, :], preferred_element_type=jnp.float32
            ) * table[panels + panel, relative].astype(jnp.float32)
            result = product if result is None else result + product
        return result

    low = 2 * z < depth

    def target(stage):
        falling = depth - 1 - stage
        of_low = jnp.where(falling > z, falling, stage - (depth - 1 - z))
        of_high = jnp.where(stage < z, stage, depth - 1 - (stage - z))
        of_stage = jnp.where(low, of_low, of_high)
        return jnp.where(stage == stages, z, of_stage)

    skipped = jnp.where(z == 0, 0, jnp.where(low, stages - 1, z - 1))

    def x_copy(group, chunk):
        return pltpu.make_async_remote_copy(
            src_ref=x_out.at[group, chunk],
            dst_ref=x_in.at[group, chunk],
            send_sem=x_send.at[group, chunk],
            recv_sem=x_recv.at[group, chunk],
            device_id={"site": site + 1 - 2 * x},
            device_id_type=MESH,
        )

    def group_of(turn):
        return jnp.where(x == 0, jnp.where(turn >= skipped, turn + 1, turn), turn)

    def x_step(step, source=factor):
        group, chunk = group_of(step // chunks), step % chunks
        offset = (PAIR * (target(group) - z + depth) + 1 - 2 * x) % (PAIR * depth)
        x_out[group, chunk] = partial(offset, chunk, source)
        x_copy(group, chunk).start()

    def z_copy(side, dest, chunk, stage, there):
        return pltpu.make_async_remote_copy(
            src_ref=z_out.at[stage, chunk],
            dst_ref=z_in.at[side, dest, chunk],
            send_sem=z_send.at[stage, chunk],
            recv_sem=z_recv.at[side, dest, chunk],
            device_id={"site": there},
            device_id_type=MESH,
        )

    def arrived(side, dest, chunk):
        z_copy(side, dest, chunk, 0, (site + PAIR) % (PAIR * depth)).wait_recv()
        return z_in[side, dest, chunk]

    def z_step(step):
        stage, chunk = step // chunks, step % chunks
        dest = target(stage)
        up = dest > z
        side = jnp.where(up, 0, 1)
        offset = PAIR * ((dest - z + depth) % depth)
        z_out[stage, chunk] = partial(offset, chunk)

        @pl.when(jnp.logical_or(x == 0, stage != skipped))
        def _():
            x_copy(stage, chunk).wait_recv()
            z_out[stage, chunk] = z_out[stage, chunk] + x_in[stage, chunk]

        @pl.when(jnp.where(up, z, depth - 1 - z) > 0)
        def _():
            z_out[stage, chunk] = z_out[stage, chunk] + arrived(side, dest, chunk)

        z_copy(side, dest, chunk, stage, jnp.where(up, site + PAIR, site - PAIR)).start()

    def last_step(chunk):
        spare = z_out.at[stages, 0]
        spare[...] = partial(0, chunk)

        @pl.when(x == 1)
        def _():
            x_copy(stages, chunk).wait_recv()
            spare[...] = spare[...] + x_in[stages, chunk]

        @pl.when(z > 0)
        def _():
            spare[...] = spare[...] + arrived(0, z, chunk)

        @pl.when(z < depth - 1)
        def _():
            spare[...] = spare[...] + arrived(1, z, chunk)

        rounded = spare[...].astype(jnp.bfloat16)
        rows = pl.ds(pl.multiple_of(chunk * ROWS, ROWS), ROWS)
        field_out[rows, :] = rounded
        folded = None
        for piece in range(own_reals // LANES):
            residual = rounded[:, piece * LANES:(piece + 1) * LANES].astype(jnp.float32)
            log_peak = columns[0, rows, :] + columns[1, rows, :] * residual
            log_ratio = columns[2, rows, :] - log_peak
            margin = jnp.maximum(1.0 - jnp.exp(log_ratio), 0.0)
            displacement = coeff_disp * jnp.exp(power_margin * jnp.log(margin) - power_ratio * log_ratio)
            damage = jnp.log1p(displacement)
            folded = damage if folded is None else folded + damage
        folds[rows, :] = folded

        @pl.when((chunk + 1) % (LANES // ROWS) == 0)
        def _():
            line = chunk // (LANES // ROWS)
            group = folds[pl.ds(pl.multiple_of(line * LANES, LANES), LANES), :]
            totals[me, pl.ds(line, 1), :] = jnp.sum(group.T, axis=0, keepdims=True)

    for step in range(HEAD):
        x_step(step, head)
    for load in rest:
        load.wait()

    @pl.loop(HEAD, AHEAD)
    def _(step):
        x_step(step)

    @pl.loop(0, steps)
    def _(step):
        @pl.when(step + AHEAD < steps)
        def _():
            x_step(step + AHEAD)

        z_step(step)

        @pl.when(step >= steps - chunks + LAG)
        def _():
            last_step(step - (steps - chunks + LAG))

    @pl.loop(chunks - LAG, chunks)
    def _(chunk):
        last_step(chunk)

    def t_copy(shift):
        return pltpu.make_async_remote_copy(
            src_ref=totals.at[me],
            dst_ref=totals.at[me],
            send_sem=t_send.at[shift],
            recv_sem=t_recv.at[shift],
            device_id={"real": (me + shift) % reals},
            device_id_type=MESH,
        )

    for shift in range(1, reals):
        t_copy(shift).start()

    @pl.loop(0, steps)
    def _(step):
        x_copy(group_of(step // chunks), step % chunks).wait_send()
        z_copy(0, 0, step % chunks, step // chunks, (site + PAIR) % (PAIR * depth)).wait_send()

    for shift in range(1, reals):
        t_copy(shift).wait()
    total = totals[0]
    for source in range(1, reals):
        total = total + totals[source]
    mean_out[...] = total / (own_reals * reals)


def hand_out_kernel(field_in, mean_in, field_out, mean_out, field, mean, in_sem, out_sem):
    part = field.shape[1]
    reads = [pltpu.make_async_copy(mean_in, mean, in_sem.at[PARTS])]
    writes = [pltpu.make_async_copy(mean, mean_out, out_sem.at[PARTS])]
    for index in range(PARTS):
        rows = pl.ds(index * part, part)
        reads.append(pltpu.make_async_copy(field_in.at[rows, :], field.at[index], in_sem.at[index]))
        writes.append(pltpu.make_async_copy(field.at[index], field_out.at[rows, :], out_sem.at[index]))
    for read in reads:
        read.start()
    for read, write in zip(reads, writes):
        read.wait()
        write.start()
    for write in writes:
        write.wait()


def line_shards(epsilon, factor, block_rows, median_log, spread_log, critical_yield):
    panels, per_column, tile = factor.shape[:3]
    sites, own_reals = epsilon.shape
    count, reals = lax.axis_size("site"), lax.axis_size("real")
    depth = count // PAIR
    chunks = sites // ROWS
    lines = sites // LANES
    piece = (ROWS, own_reals)
    vmem = pl.BlockSpec(memory_space=pltpu.VMEM)
    anywhere = pl.BlockSpec(memory_space=pl.ANY)
    field, mean = pl.pallas_call(
        functools.partial(field_kernel, depth, own_reals),
        out_shape=(
            jax.ShapeDtypeStruct((sites, own_reals), jnp.bfloat16),
            jax.ShapeDtypeStruct((lines, LANES), jnp.float32),
        ),
        in_specs=[pl.BlockSpec(memory_space=pltpu.SMEM), anywhere, anywhere, vmem, vmem, vmem],
        out_specs=(vmem, vmem),
        scratch_shapes=[
            pltpu.VMEM(epsilon.shape, epsilon.dtype),
            pltpu.VMEM(factor.shape, factor.dtype),
            pltpu.VMEM((panels, per_column, HEAD * ROWS, tile), factor.dtype),
            pltpu.VMEM((depth, chunks) + piece, jnp.float32),
            pltpu.VMEM((depth, chunks) + piece, jnp.float32),
            pltpu.VMEM((depth, chunks) + piece, jnp.float32),
            pltpu.VMEM((2, depth, chunks) + piece, jnp.float32),
            pltpu.VMEM((reals, lines, LANES), jnp.float32),
            pltpu.VMEM((3, sites, LANES), jnp.float32),
            pltpu.VMEM((sites, LANES), jnp.float32),
            pltpu.SMEM((2 * panels, (BAND // 2 + 1) * panels), jnp.int32),
            pltpu.SemaphoreType.DMA((1 + 2 * panels,)),
            pltpu.SemaphoreType.DMA((depth, chunks)),
            pltpu.SemaphoreType.DMA((depth, chunks)),
            pltpu.SemaphoreType.DMA((depth, chunks)),
            pltpu.SemaphoreType.DMA((2, depth, chunks)),
            pltpu.SemaphoreType.DMA((reals,)),
            pltpu.SemaphoreType.DMA((reals,)),
        ],
        compiler_params=pltpu.CompilerParams(
            collective_id=0, has_side_effects=True, vmem_limit_bytes=60 * 1024 * 1024
        ),
    )(
        block_rows,
        epsilon,
        factor,
        median_log.reshape(lines, LANES),
        spread_log.reshape(lines, LANES),
        critical_yield.reshape(lines, LANES),
    )
    field, mean = pl.pallas_call(
        hand_out_kernel,
        out_shape=(
            jax.ShapeDtypeStruct(field.shape, field.dtype),
            jax.ShapeDtypeStruct(mean.shape, mean.dtype),
        ),
        in_specs=[anywhere, anywhere],
        out_specs=(anywhere, anywhere),
        scratch_shapes=[
            pltpu.VMEM((PARTS, sites // PARTS, own_reals), field.dtype),
            pltpu.VMEM(mean.shape, mean.dtype),
            pltpu.SemaphoreType.DMA((PARTS + 1,)),
            pltpu.SemaphoreType.DMA((PARTS + 1,)),
        ],
    )(field, mean)
    return field, mean.reshape(sites)


def solution(mesh):
    body = line_shards if mesh.shape["site"] == BAND // 2 + PAIR else shards
    return jax.shard_map(
        body,
        mesh=mesh,
        in_specs=(
            P("site", "real"),
            P(None, "site", None, None),
            P(None, "site"),
            P("site"),
            P("site"),
            P("site"),
        ),
        out_specs=(P("site", "real"), P("site")),
        check_vma=False,
    )
```

```python
import functools
import jax
import jax.numpy as jnp
from jax import lax
from jax.experimental import pallas as pl
from jax.experimental.pallas import tpu as pltpu
from jax.sharding import PartitionSpec as P

BAND = 12
PAIR = 2
LANES = 128
ROWS = 64
AHEAD = 6
PARTS = 4
HEAD = 2
LAG = 1
MESH = pl.DeviceIdType.MESH

coeff_disp = 10.0**0.215
power_margin = 2.341
power_ratio = 1.438


def passed_along(value, axis, steps):
    count = lax.axis_size(axis)
    pairs = [(source, (source + steps) % count) for source in range(count)]
    return lax.ppermute(value, axis, pairs)


def shards(epsilon, factor, block_rows, median_log, spread_log, critical_yield):
    panels = factor.shape[0]
    per_column = factor.shape[1]
    tile_size = factor.shape[-1]
    own_reals = epsilon.shape[1]
    reach = BAND // 2
    own_index = lax.axis_index("site")
    total_tiles = panels * lax.axis_size("site")
    draws = epsilon.reshape(panels, tile_size, own_reals)

    def pending(panel):
        flat = factor[panel].reshape(per_column * tile_size, tile_size)
        products = jnp.dot(flat, draws[panel], preferred_element_type=jnp.float32)
        products = products.reshape(per_column, tile_size, own_reals)
        relative = (block_rows[panel] - own_index * panels) % total_tiles
        slots = jnp.zeros(((reach + 1) * panels, tile_size, own_reals), jnp.float32)
        sums = slots.at[relative].set(products, unique_indices=True)
        return sums.reshape(reach + 1, panels, tile_size, own_reals)

    combined = pending(0)
    panel = 1
    combined = combined + pending(panel)
    arrived = combined[0]
    for offset in range(1, reach + 1):
        arrived = arrived + passed_along(combined[offset], "site", offset)
    residual_field = arrived.astype(jnp.bfloat16).reshape(panels * tile_size, own_reals)
    log_peak = median_log[:, None] + spread_log[:, None] * residual_field.astype(jnp.float32)
    log_ratio = jnp.log(critical_yield)[:, None] - log_peak
    ratio = jnp.exp(log_ratio)
    margin = jnp.maximum(1.0 - ratio, 0.0)
    displacement = coeff_disp * jnp.power(margin, power_margin) * jnp.exp(-power_ratio * log_ratio)
    local_total = jnp.sum(jnp.log1p(displacement), axis=1)
    total = lax.psum(local_total, "real")
    mean_damage = total / (own_reals * lax.axis_size("real"))
    return (residual_field, mean_damage)


def field_kernel(
    depth, own_reals, block_rows, eps_in, factor_in, median, spread, critical, field_out, mean_out,
    eps, factor, head, x_out, x_in, z_out, z_in, totals, columns, folds, table,
    load_sem, x_send, x_recv, z_send, z_recv, t_send, t_recv,
):
    panels, per_column, tile = factor.shape[0], factor.shape[1], factor.shape[2]
    chunks = panels * tile // ROWS
    per_tile = tile // ROWS
    stages = depth - 1
    steps = stages * chunks
    reals = lax.axis_size("real")
    site = lax.axis_index("site")
    me = lax.axis_index("real")
    z, x = site // PAIR, site % PAIR

    first = [pltpu.make_async_copy(eps_in, eps, load_sem.at[0])]
    rest = []
    for panel in range(panels):
        first.append(pltpu.make_async_copy(
            factor_in.at[panel, :, :head.shape[2], :], head.at[panel], load_sem.at[1 + panel]
        ))
        rest.append(pltpu.make_async_copy(
            factor_in.at[panel], factor.at[panel], load_sem.at[1 + panels + panel]
        ))
    for load in first + rest:
        load.start()

    barrier = pltpu.get_barrier_semaphore()
    pl.semaphore_signal(barrier, inc=1, device_id={"site": site + 1 - 2 * x}, device_id_type=MESH)
    for shift in range(1, reals):
        pl.semaphore_signal(barrier, inc=1, device_id={"real": (me + shift) % reals}, device_id_type=MESH)

    @pl.when(z > 0)
    def _():
        pl.semaphore_signal(barrier, inc=1, device_id={"site": site - PAIR}, device_id_type=MESH)

    @pl.when(z < depth - 1)
    def _():
        pl.semaphore_signal(barrier, inc=1, device_id={"site": site + PAIR}, device_id_type=MESH)

    for panel in range(panels):
        begins = [
            (block_rows[panel, block] - site * panels + panels * PAIR * depth) % (panels * PAIR * depth)
            for block in range(per_column)
        ]

        @pl.loop(0, table.shape[1])
        def _(slot):
            number, found = jnp.int32(0), jnp.int32(0)
            for block in range(per_column):
                hit = begins[block] == slot
                number = jnp.where(hit, block, number)
                found = jnp.where(hit, 1, found)
            table[panel, slot] = number
            table[panels + panel, slot] = found

    pl.semaphore_wait(barrier, reals + jnp.where(z > 0, 1, 0) + jnp.where(z < depth - 1, 1, 0))

    for load in first:
        load.wait()

    def partial(offset, chunk, source=factor):
        relative = panels * offset + chunk // per_tile
        row = pl.multiple_of((chunk % per_tile) * ROWS, ROWS)
        result = None
        for panel in range(panels):
            block = source[panel, table[panel, relative], pl.ds(row, ROWS), :]
            product = jnp.dot(
                block, eps[panel * tile:(panel + 1) * tile, :], preferred_element_type=jnp.float32
            ) * table[panels + panel, relative].astype(jnp.float32)
            result = product if result is None else result + product
        return result

    low = 2 * z < depth

    def target(stage):
        falling = depth - 1 - stage
        of_low = jnp.where(falling > z, falling, stage - (depth - 1 - z))
        of_high = jnp.where(stage < z, stage, depth - 1 - (stage - z))
        of_stage = jnp.where(low, of_low, of_high)
        return jnp.where(stage == stages, z, of_stage)

    skipped = jnp.where(z == 0, 0, jnp.where(low, stages - 1, z - 1))

    def x_copy(group, chunk):
        return pltpu.make_async_remote_copy(
            src_ref=x_out.at[group, chunk],
            dst_ref=x_in.at[group, chunk],
            send_sem=x_send.at[group, chunk],
            recv_sem=x_recv.at[group, chunk],
            device_id={"site": site + 1 - 2 * x},
            device_id_type=MESH,
        )

    def group_of(turn):
        return jnp.where(x == 0, jnp.where(turn >= skipped, turn + 1, turn), turn)

    def x_step(step, source=factor):
        group, chunk = group_of(step // chunks), step % chunks
        offset = (PAIR * (target(group) - z + depth) + 1 - 2 * x) % (PAIR * depth)
        x_out[group, chunk] = partial(offset, chunk, source)
        x_copy(group, chunk).start()

    def z_copy(side, dest, chunk, stage, there):
        return pltpu.make_async_remote_copy(
            src_ref=z_out.at[stage, chunk],
            dst_ref=z_in.at[side, dest, chunk],
            send_sem=z_send.at[stage, chunk],
            recv_sem=z_recv.at[side, dest, chunk],
            device_id={"site": there},
            device_id_type=MESH,
        )

    def arrived(side, dest, chunk):
        z_copy(side, dest, chunk, 0, (site + PAIR) % (PAIR * depth)).wait_recv()
        return z_in[side, dest, chunk]

    def z_step(step):
        stage, chunk = step // chunks, step % chunks
        dest = target(stage)
        up = dest > z
        side = jnp.where(up, 0, 1)
        offset = PAIR * ((dest - z + depth) % depth)
        z_out[stage, chunk] = partial(offset, chunk)

        @pl.when(jnp.logical_or(x == 0, stage != skipped))
        def _():
            x_copy(stage, chunk).wait_recv()
            z_out[stage, chunk] = z_out[stage, chunk] + x_in[stage, chunk]

        @pl.when(jnp.where(up, z, depth - 1 - z) > 0)
        def _():
            z_out[stage, chunk] = z_out[stage, chunk] + arrived(side, dest, chunk)

        z_copy(side, dest, chunk, stage, jnp.where(up, site + PAIR, site - PAIR)).start()

    def last_step(chunk):
        spare = z_out.at[stages, 0]
        spare[...] = partial(0, chunk)

        @pl.when(x == 1)
        def _():
            x_copy(stages, chunk).wait_recv()
            spare[...] = spare[...] + x_in[stages, chunk]

        @pl.when(z > 0)
        def _():
            spare[...] = spare[...] + arrived(0, z, chunk)

        @pl.when(z < depth - 1)
        def _():
            spare[...] = spare[...] + arrived(1, z, chunk)

        rounded = spare[...].astype(jnp.bfloat16)
        rows = pl.ds(pl.multiple_of(chunk * ROWS, ROWS), ROWS)
        field_out[rows, :] = rounded
        folded = None
        for piece in range(own_reals // LANES):
            residual = rounded[:, piece * LANES:(piece + 1) * LANES].astype(jnp.float32)
            log_peak = columns[0, rows, :] + columns[1, rows, :] * residual
            log_ratio = columns[2, rows, :] - log_peak
            margin = jnp.maximum(1.0 - jnp.exp(log_ratio), 0.0)
            displacement = coeff_disp * jnp.exp(power_margin * jnp.log(margin) - power_ratio * log_ratio)
            damage = jnp.log1p(displacement)
            folded = damage if folded is None else folded + damage
        folds[rows, :] = folded

        @pl.when((chunk + 1) % (LANES // ROWS) == 0)
        def _():
            line = chunk // (LANES // ROWS)
            group = folds[pl.ds(pl.multiple_of(line * LANES, LANES), LANES), :]
            totals[me, pl.ds(line, 1), :] = jnp.sum(group.T, axis=0, keepdims=True)

    for step in range(HEAD):
        x_step(step, head)
    for load in rest:
        load.wait()

    @pl.loop(HEAD, AHEAD)
    def _(step):
        x_step(step)

    for index, ref in enumerate((median, spread, critical)):
        for line in range(panels * tile // LANES):
            spot = slice(line * LANES, (line + 1) * LANES)
            value = ref[line:line + 1, :]
            value = jnp.log(value) if index == 2 else value
            columns[index, spot, :] = jnp.broadcast_to(value, (LANES, LANES)).T

    @pl.loop(0, steps)
    def _(step):
        @pl.when(step + AHEAD < steps)
        def _():
            x_step(step + AHEAD)

        z_step(step)

        @pl.when(step >= steps - chunks + LAG)
        def _():
            last_step(step - (steps - chunks + LAG))

    @pl.loop(chunks - LAG, chunks)
    def _(chunk):
        last_step(chunk)

    def t_copy(shift):
        return pltpu.make_async_remote_copy(
            src_ref=totals.at[me],
            dst_ref=totals.at[me],
            send_sem=t_send.at[shift],
            recv_sem=t_recv.at[shift],
            device_id={"real": (me + shift) % reals},
            device_id_type=MESH,
        )

    for shift in range(1, reals):
        t_copy(shift).start()

    @pl.loop(0, steps)
    def _(step):
        x_copy(group_of(step // chunks), step % chunks).wait_send()
        z_copy(0, 0, step % chunks, step // chunks, (site + PAIR) % (PAIR * depth)).wait_send()

    for shift in range(1, reals):
        t_copy(shift).wait()
    total = totals[0]
    for source in range(1, reals):
        total = total + totals[source]
    mean_out[...] = total / (own_reals * reals)


def hand_out_kernel(field_in, mean_in, field_out, mean_out, field, mean, in_sem, out_sem):
    part = field.shape[1]
    reads = [pltpu.make_async_copy(mean_in, mean, in_sem.at[PARTS])]
    writes = [pltpu.make_async_copy(mean, mean_out, out_sem.at[PARTS])]
    for index in range(PARTS):
        rows = pl.ds(index * part, part)
        reads.append(pltpu.make_async_copy(field_in.at[rows, :], field.at[index], in_sem.at[index]))
        writes.append(pltpu.make_async_copy(field.at[index], field_out.at[rows, :], out_sem.at[index]))
    for read in reads:
        read.start()
    for read, write in zip(reads, writes):
        read.wait()
        write.start()
    for write in writes:
        write.wait()


def line_shards(epsilon, factor, block_rows, median_log, spread_log, critical_yield):
    panels, per_column, tile = factor.shape[:3]
    sites, own_reals = epsilon.shape
    count, reals = lax.axis_size("site"), lax.axis_size("real")
    depth = count // PAIR
    chunks = sites // ROWS
    lines = sites // LANES
    piece = (ROWS, own_reals)
    vmem = pl.BlockSpec(memory_space=pltpu.VMEM)
    anywhere = pl.BlockSpec(memory_space=pl.ANY)
    field, mean = pl.pallas_call(
        functools.partial(field_kernel, depth, own_reals),
        out_shape=(
            jax.ShapeDtypeStruct((sites, own_reals), jnp.bfloat16),
            jax.ShapeDtypeStruct((lines, LANES), jnp.float32),
        ),
        in_specs=[pl.BlockSpec(memory_space=pltpu.SMEM), anywhere, anywhere, vmem, vmem, vmem],
        out_specs=(vmem, vmem),
        scratch_shapes=[
            pltpu.VMEM(epsilon.shape, epsilon.dtype),
            pltpu.VMEM(factor.shape, factor.dtype),
            pltpu.VMEM((panels, per_column, HEAD * ROWS, tile), factor.dtype),
            pltpu.VMEM((depth, chunks) + piece, jnp.float32),
            pltpu.VMEM((depth, chunks) + piece, jnp.float32),
            pltpu.VMEM((depth, chunks) + piece, jnp.float32),
            pltpu.VMEM((2, depth, chunks) + piece, jnp.float32),
            pltpu.VMEM((reals, lines, LANES), jnp.float32),
            pltpu.VMEM((3, sites, LANES), jnp.float32),
            pltpu.VMEM((sites, LANES), jnp.float32),
            pltpu.SMEM((2 * panels, (BAND // 2 + 1) * panels), jnp.int32),
            pltpu.SemaphoreType.DMA((1 + 2 * panels,)),
            pltpu.SemaphoreType.DMA((depth, chunks)),
            pltpu.SemaphoreType.DMA((depth, chunks)),
            pltpu.SemaphoreType.DMA((depth, chunks)),
            pltpu.SemaphoreType.DMA((2, depth, chunks)),
            pltpu.SemaphoreType.DMA((reals,)),
            pltpu.SemaphoreType.DMA((reals,)),
        ],
        compiler_params=pltpu.CompilerParams(
            collective_id=0, has_side_effects=True, vmem_limit_bytes=60 * 1024 * 1024
        ),
    )(
        block_rows,
        epsilon,
        factor,
        median_log.reshape(lines, LANES),
        spread_log.reshape(lines, LANES),
        critical_yield.reshape(lines, LANES),
    )
    field, mean = pl.pallas_call(
        hand_out_kernel,
        out_shape=(
            jax.ShapeDtypeStruct(field.shape, field.dtype),
            jax.ShapeDtypeStruct(mean.shape, mean.dtype),
        ),
        in_specs=[anywhere, anywhere],
        out_specs=(anywhere, anywhere),
        scratch_shapes=[
            pltpu.VMEM((PARTS, sites // PARTS, own_reals), field.dtype),
            pltpu.VMEM(mean.shape, mean.dtype),
            pltpu.SemaphoreType.DMA((PARTS + 1,)),
            pltpu.SemaphoreType.DMA((PARTS + 1,)),
        ],
    )(field, mean)
    return field, mean.reshape(sites)


def solution(mesh):
    body = line_shards if mesh.shape["site"] == BAND // 2 + PAIR else shards
    return jax.shard_map(
        body,
        mesh=mesh,
        in_specs=(
            P("site", "real"),
            P(None, "site", None, None),
            P(None, "site"),
            P("site"),
            P("site"),
            P("site"),
        ),
        out_specs=(P("site", "real"), P("site")),
        check_vma=False,
    )
```

```python
import functools
import jax
import jax.numpy as jnp
from jax import lax
from jax.experimental import pallas as pl
from jax.experimental.pallas import tpu as pltpu
from jax.sharding import PartitionSpec as P

BAND = 12
PAIR = 2
LANES = 128
ROWS = 64
AHEAD = 6
PARTS = 4
HEAD = 2
LAG = 1
MESH = pl.DeviceIdType.MESH

coeff_disp = 10.0**0.215
power_margin = 2.341
power_ratio = 1.438


def passed_along(value, axis, steps):
    count = lax.axis_size(axis)
    pairs = [(source, (source + steps) % count) for source in range(count)]
    return lax.ppermute(value, axis, pairs)


def shards(epsilon, factor, block_rows, median_log, spread_log, critical_yield):
    panels = factor.shape[0]
    per_column = factor.shape[1]
    tile_size = factor.shape[-1]
    own_reals = epsilon.shape[1]
    reach = BAND // 2
    own_index = lax.axis_index("site")
    total_tiles = panels * lax.axis_size("site")
    draws = epsilon.reshape(panels, tile_size, own_reals)

    def pending(panel):
        flat = factor[panel].reshape(per_column * tile_size, tile_size)
        products = jnp.dot(flat, draws[panel], preferred_element_type=jnp.float32)
        products = products.reshape(per_column, tile_size, own_reals)
        relative = (block_rows[panel] - own_index * panels) % total_tiles
        slots = jnp.zeros(((reach + 1) * panels, tile_size, own_reals), jnp.float32)
        sums = slots.at[relative].set(products, unique_indices=True)
        return sums.reshape(reach + 1, panels, tile_size, own_reals)

    combined = pending(0)
    panel = 1
    combined = combined + pending(panel)
    arrived = combined[0]
    for offset in range(1, reach + 1):
        arrived = arrived + passed_along(combined[offset], "site", offset)
    residual_field = arrived.astype(jnp.bfloat16).reshape(panels * tile_size, own_reals)
    log_peak = median_log[:, None] + spread_log[:, None] * residual_field.astype(jnp.float32)
    log_ratio = jnp.log(critical_yield)[:, None] - log_peak
    ratio = jnp.exp(log_ratio)
    margin = jnp.maximum(1.0 - ratio, 0.0)
    displacement = coeff_disp * jnp.power(margin, power_margin) * jnp.exp(-power_ratio * log_ratio)
    local_total = jnp.sum(jnp.log1p(displacement), axis=1)
    total = lax.psum(local_total, "real")
    mean_damage = total / (own_reals * lax.axis_size("real"))
    return (residual_field, mean_damage)


def field_kernel(
    depth, own_reals, block_rows, eps_in, factor_in, median, spread, critical, field_out, mean_out,
    eps, factor, head, x_out, x_in, z_out, z_in, totals, columns, folds, table, field,
    load_sem, x_send, x_recv, z_send, z_recv, t_send, t_recv, f_send,
):
    panels, per_column, tile = factor.shape[0], factor.shape[1], factor.shape[2]
    chunks = panels * tile // ROWS
    per_tile = tile // ROWS
    stages = depth - 1
    steps = stages * chunks
    reals = lax.axis_size("real")
    site = lax.axis_index("site")
    me = lax.axis_index("real")
    z, x = site // PAIR, site % PAIR

    first = [pltpu.make_async_copy(eps_in, eps, load_sem.at[0])]
    rest = []
    for panel in range(panels):
        first.append(pltpu.make_async_copy(
            factor_in.at[panel, :, :head.shape[2], :], head.at[panel], load_sem.at[1 + panel]
        ))
        rest.append(pltpu.make_async_copy(
            factor_in.at[panel], factor.at[panel], load_sem.at[1 + panels + panel]
        ))
    for load in first + rest:
        load.start()

    barrier = pltpu.get_barrier_semaphore()
    pl.semaphore_signal(barrier, inc=1, device_id={"site": site + 1 - 2 * x}, device_id_type=MESH)
    for shift in range(1, reals):
        pl.semaphore_signal(barrier, inc=1, device_id={"real": (me + shift) % reals}, device_id_type=MESH)

    @pl.when(z > 0)
    def _():
        pl.semaphore_signal(barrier, inc=1, device_id={"site": site - PAIR}, device_id_type=MESH)

    @pl.when(z < depth - 1)
    def _():
        pl.semaphore_signal(barrier, inc=1, device_id={"site": site + PAIR}, device_id_type=MESH)

    for panel in range(panels):
        begins = [
            (block_rows[panel, block] - site * panels + panels * PAIR * depth) % (panels * PAIR * depth)
            for block in range(per_column)
        ]

        @pl.loop(0, table.shape[1])
        def _(slot):
            number, found = jnp.int32(0), jnp.int32(0)
            for block in range(per_column):
                hit = begins[block] == slot
                number = jnp.where(hit, block, number)
                found = jnp.where(hit, 1, found)
            table[panel, slot] = number
            table[panels + panel, slot] = found

    pl.semaphore_wait(barrier, reals + jnp.where(z > 0, 1, 0) + jnp.where(z < depth - 1, 1, 0))

    for load in first:
        load.wait()

    def partial(offset, chunk, source=factor):
        relative = panels * offset + chunk // per_tile
        row = pl.multiple_of((chunk % per_tile) * ROWS, ROWS)
        result = None
        for panel in range(panels):
            block = source[panel, table[panel, relative], pl.ds(row, ROWS), :]
            product = jnp.dot(
                block, eps[panel * tile:(panel + 1) * tile, :], preferred_element_type=jnp.float32
            ) * table[panels + panel, relative].astype(jnp.float32)
            result = product if result is None else result + product
        return result

    low = 2 * z < depth

    def target(stage):
        falling = depth - 1 - stage
        of_low = jnp.where(falling > z, falling, stage - (depth - 1 - z))
        of_high = jnp.where(stage < z, stage, depth - 1 - (stage - z))
        of_stage = jnp.where(low, of_low, of_high)
        return jnp.where(stage == stages, z, of_stage)

    skipped = jnp.where(z == 0, 0, jnp.where(low, stages - 1, z - 1))

    def x_copy(group, chunk):
        return pltpu.make_async_remote_copy(
            src_ref=x_out.at[group, chunk],
            dst_ref=x_in.at[group, chunk],
            send_sem=x_send.at[group, chunk],
            recv_sem=x_recv.at[group, chunk],
            device_id={"site": site + 1 - 2 * x},
            device_id_type=MESH,
        )

    def group_of(turn):
        return jnp.where(x == 0, jnp.where(turn >= skipped, turn + 1, turn), turn)

    def x_step(step, source=factor):
        group, chunk = group_of(step // chunks), step % chunks
        offset = (PAIR * (target(group) - z + depth) + 1 - 2 * x) % (PAIR * depth)
        x_out[group, chunk] = partial(offset, chunk, source)
        x_copy(group, chunk).start()

    def z_copy(side, dest, chunk, stage, there):
        return pltpu.make_async_remote_copy(
            src_ref=z_out.at[stage, chunk],
            dst_ref=z_in.at[side, dest, chunk],
            send_sem=z_send.at[stage, chunk],
            recv_sem=z_recv.at[side, dest, chunk],
            device_id={"site": there},
            device_id_type=MESH,
        )

    def arrived(side, dest, chunk):
        z_copy(side, dest, chunk, 0, (site + PAIR) % (PAIR * depth)).wait_recv()
        return z_in[side, dest, chunk]

    def z_step(step):
        stage, chunk = step // chunks, step % chunks
        dest = target(stage)
        up = dest > z
        side = jnp.where(up, 0, 1)
        offset = PAIR * ((dest - z + depth) % depth)
        z_out[stage, chunk] = partial(offset, chunk)

        @pl.when(jnp.logical_or(x == 0, stage != skipped))
        def _():
            x_copy(stage, chunk).wait_recv()
            z_out[stage, chunk] = z_out[stage, chunk] + x_in[stage, chunk]

        @pl.when(jnp.where(up, z, depth - 1 - z) > 0)
        def _():
            z_out[stage, chunk] = z_out[stage, chunk] + arrived(side, dest, chunk)

        z_copy(side, dest, chunk, stage, jnp.where(up, site + PAIR, site - PAIR)).start()

    def field_copy(chunk):
        rows = pl.ds(pl.multiple_of(chunk * ROWS, ROWS), ROWS)
        return pltpu.make_async_copy(field.at[chunk], field_out.at[rows, :], f_send.at[chunk])

    def last_step(chunk):
        spare = z_out.at[stages, 0]
        spare[...] = partial(0, chunk)

        @pl.when(x == 1)
        def _():
            x_copy(stages, chunk).wait_recv()
            spare[...] = spare[...] + x_in[stages, chunk]

        @pl.when(z > 0)
        def _():
            spare[...] = spare[...] + arrived(0, z, chunk)

        @pl.when(z < depth - 1)
        def _():
            spare[...] = spare[...] + arrived(1, z, chunk)

        rounded = spare[...].astype(jnp.bfloat16)
        rows = pl.ds(pl.multiple_of(chunk * ROWS, ROWS), ROWS)
        field[chunk] = rounded
        field_copy(chunk).start()
        folded = None
        for piece in range(own_reals // LANES):
            residual = rounded[:, piece * LANES:(piece + 1) * LANES].astype(jnp.float32)
            log_peak = columns[0, rows, :] + columns[1, rows, :] * residual
            log_ratio = columns[2, rows, :] - log_peak
            margin = jnp.maximum(1.0 - jnp.exp(log_ratio), 0.0)
            displacement = coeff_disp * jnp.exp(power_margin * jnp.log(margin) - power_ratio * log_ratio)
            damage = jnp.log1p(displacement)
            folded = damage if folded is None else folded + damage
        folds[rows, :] = folded

        @pl.when((chunk + 1) % (LANES // ROWS) == 0)
        def _():
            line = chunk // (LANES // ROWS)
            group = folds[pl.ds(pl.multiple_of(line * LANES, LANES), LANES), :]
            totals[me, pl.ds(line, 1), :] = jnp.sum(group.T, axis=0, keepdims=True)

    for step in range(HEAD):
        x_step(step, head)
    for load in rest:
        load.wait()

    @pl.loop(HEAD, AHEAD)
    def _(step):
        x_step(step)

    @pl.loop(0, steps)
    def _(step):
        @pl.when(step + AHEAD < steps)
        def _():
            x_step(step + AHEAD)

        z_step(step)

        @pl.when(step < panels * tile // LANES)
        def _():
            spot = pl.ds(pl.multiple_of(step * LANES, LANES), LANES)
            for index, ref in enumerate((median, spread, critical)):
                value = ref[pl.ds(step, 1), :]
                value = jnp.log(value) if index == 2 else value
                columns[index, spot, :] = jnp.broadcast_to(value, (LANES, LANES)).T

        @pl.when(step >= steps - chunks + LAG)
        def _():
            last_step(step - (steps - chunks + LAG))

    @pl.loop(chunks - LAG, chunks)
    def _(chunk):
        last_step(chunk)

    def t_copy(shift):
        return pltpu.make_async_remote_copy(
            src_ref=totals.at[me],
            dst_ref=totals.at[me],
            send_sem=t_send.at[shift],
            recv_sem=t_recv.at[shift],
            device_id={"real": (me + shift) % reals},
            device_id_type=MESH,
        )

    for shift in range(1, reals):
        t_copy(shift).start()

    @pl.loop(0, steps)
    def _(step):
        x_copy(group_of(step // chunks), step % chunks).wait_send()
        z_copy(0, 0, step % chunks, step // chunks, (site + PAIR) % (PAIR * depth)).wait_send()

    @pl.loop(0, chunks)
    def _(chunk):
        field_copy(chunk).wait()

    for shift in range(1, reals):
        t_copy(shift).wait()
    total = totals[0]
    for source in range(1, reals):
        total = total + totals[source]
    mean_out[...] = total / (own_reals * reals)


def hand_out_kernel(field_in, mean_in, field_out, mean_out, field, mean, in_sem, out_sem):
    part = field.shape[1]
    reads = [pltpu.make_async_copy(mean_in, mean, in_sem.at[PARTS])]
    writes = [pltpu.make_async_copy(mean, mean_out, out_sem.at[PARTS])]
    for index in range(PARTS):
        rows = pl.ds(index * part, part)
        reads.append(pltpu.make_async_copy(field_in.at[rows, :], field.at[index], in_sem.at[index]))
        writes.append(pltpu.make_async_copy(field.at[index], field_out.at[rows, :], out_sem.at[index]))
    for read in reads:
        read.start()
    for read, write in zip(reads, writes):
        read.wait()
        write.start()
    for write in writes:
        write.wait()


def line_shards(epsilon, factor, block_rows, median_log, spread_log, critical_yield):
    panels, per_column, tile = factor.shape[:3]
    sites, own_reals = epsilon.shape
    count, reals = lax.axis_size("site"), lax.axis_size("real")
    depth = count // PAIR
    chunks = sites // ROWS
    lines = sites // LANES
    piece = (ROWS, own_reals)
    vmem = pl.BlockSpec(memory_space=pltpu.VMEM)
    anywhere = pl.BlockSpec(memory_space=pl.ANY)
    field, mean = pl.pallas_call(
        functools.partial(field_kernel, depth, own_reals),
        out_shape=(
            jax.ShapeDtypeStruct((sites, own_reals), jnp.bfloat16),
            jax.ShapeDtypeStruct((lines, LANES), jnp.float32),
        ),
        in_specs=[pl.BlockSpec(memory_space=pltpu.SMEM), anywhere, anywhere, vmem, vmem, vmem],
        out_specs=(anywhere, vmem),
        scratch_shapes=[
            pltpu.VMEM(epsilon.shape, epsilon.dtype),
            pltpu.VMEM(factor.shape, factor.dtype),
            pltpu.VMEM((panels, per_column, HEAD * ROWS, tile), factor.dtype),
            pltpu.VMEM((depth, chunks) + piece, jnp.float32),
            pltpu.VMEM((depth, chunks) + piece, jnp.float32),
            pltpu.VMEM((depth, chunks) + piece, jnp.float32),
            pltpu.VMEM((2, depth, chunks) + piece, jnp.float32),
            pltpu.VMEM((reals, lines, LANES), jnp.float32),
            pltpu.VMEM((3, sites, LANES), jnp.float32),
            pltpu.VMEM((sites, LANES), jnp.float32),
            pltpu.SMEM((2 * panels, (BAND // 2 + 1) * panels), jnp.int32),
            pltpu.VMEM((chunks, ROWS, own_reals), jnp.bfloat16),
            pltpu.SemaphoreType.DMA((1 + 2 * panels,)),
            pltpu.SemaphoreType.DMA((depth, chunks)),
            pltpu.SemaphoreType.DMA((depth, chunks)),
            pltpu.SemaphoreType.DMA((depth, chunks)),
            pltpu.SemaphoreType.DMA((2, depth, chunks)),
            pltpu.SemaphoreType.DMA((reals,)),
            pltpu.SemaphoreType.DMA((reals,)),
            pltpu.SemaphoreType.DMA((chunks,)),
        ],
        compiler_params=pltpu.CompilerParams(
            collective_id=0, has_side_effects=True, vmem_limit_bytes=60 * 1024 * 1024
        ),
    )(
        block_rows,
        epsilon,
        factor,
        median_log.reshape(lines, LANES),
        spread_log.reshape(lines, LANES),
        critical_yield.reshape(lines, LANES),
    )
    field, mean = pl.pallas_call(
        hand_out_kernel,
        out_shape=(
            jax.ShapeDtypeStruct(field.shape, field.dtype),
            jax.ShapeDtypeStruct(mean.shape, mean.dtype),
        ),
        in_specs=[anywhere, anywhere],
        out_specs=(anywhere, anywhere),
        scratch_shapes=[
            pltpu.VMEM((PARTS, sites // PARTS, own_reals), field.dtype),
            pltpu.VMEM(mean.shape, mean.dtype),
            pltpu.SemaphoreType.DMA((PARTS + 1,)),
            pltpu.SemaphoreType.DMA((PARTS + 1,)),
        ],
    )(field, mean)
    return field, mean.reshape(sites)


def solution(mesh):
    body = line_shards if mesh.shape["site"] == BAND // 2 + PAIR else shards
    return jax.shard_map(
        body,
        mesh=mesh,
        in_specs=(
            P("site", "real"),
            P(None, "site", None, None),
            P(None, "site"),
            P("site"),
            P("site"),
            P("site"),
        ),
        out_specs=(P("site", "real"), P("site")),
        check_vma=False,
    )
```
